128 devices in a mesh: row: 8 (over z, core), col: 16 (over x, y).
Axes of the slice: x: 4, y: 4, z: 4, core: 2. Of those that a mesh axis runs over, the one named last changes fastest.
Arguments:
- hessian_inverse: float32 [12288, 12288], P('row', 'col'), as said below
- weight: bfloat16 [12288, 4096], P('row', 'col'), may hold values from -6 to 6
- pruned: int32 [2, 512], replicated, may hold values from 0 to 12287, as said below
Outputs:
- hessian_after: float32 [12288, 12288], P('row', 'col')
- weight_after: bfloat16 [12288, 4096], P('row', 'col')
The draws below stay inside these ranges and needn't reach their ends.
Inputs may be any that keep to these rules, and one draw needn't show every extreme that they name: `hessian_inverse`: symmetric and positive definite. `pruned`: all 1024 channel numbers are distinct.
All inputs are finite; a program needn't handle non-finite values.
Results may differ from the reference program's by a relative error of at most 0.001.
Values sent between devices are 32-bit elements; how exact they have to be, the bound alone decides.
No kernel may reach another device: no remote copies, remote signals or barrier semaphores. Data moves between devices by JAX's collectives and lax.ppermute only.
A program may use at most 128 MiB of HBM per device.

```python
import jax
import jax.numpy as jnp
from jax import lax

N = 12288
OUT = 4096
PANEL = 512
PANELS = 2


def draw_hessian_inverse(key, part):
    inner = 1024
    first, second = jax.random.split(key)
    factors = jax.random.normal(first, (N, inner), jnp.float32)
    scales = jnp.exp(jax.random.uniform(second, (N,), jnp.float32, -0.35, 0.35))
    kernel = jnp.dot(factors, factors.T, precision=lax.Precision.HIGHEST, preferred_element_type=jnp.float32) / inner
    kernel = 0.5 * (kernel + kernel.T)
    diag_ids = jnp.arange(N)
    kernel = kernel.at[diag_ids, diag_ids].add(0.3)
    return kernel * scales[:, None] * scales[None, :]


def draw_pruned(key, part):
    order = jax.random.permutation(key, N)
    return order[:PANELS * PANEL].reshape(PANELS, PANEL).astype(jnp.int32)


def steps_of(own_key, shape, cuts, smallest, high):
    def one(position, shards_of):
        heights = jax.random.uniform(jax.random.fold_in(jax.random.fold_in(own_key, 6), position), (shards_of,), jnp.float32, smallest / len(cuts), high / len(cuts))
        return jnp.repeat(jnp.exp(heights), shape[position] // shards_of).reshape((-1,) + (1,) * (len(shape) - position - 1))

    gain = one(*cuts[0])
    for cut in cuts[1:]:
        gain = gain * one(*cut)
    return gain


def normal_values(rng, shape, scale, bound, shards=(), dtype=jnp.bfloat16):
    drawn = scale * jax.random.normal(rng, shape, jnp.float32)
    if shards:
        drawn = drawn * steps_of(rng, shape, shards, -0.22, 0.18)
    return jnp.clip(drawn, -bound, bound).astype(dtype)


def setup_inputs(seed: int = 0) -> dict:
    seeds = jax.random.split(jax.random.key(seed), 4)
    hessian_inverse = draw_hessian_inverse(jax.random.fold_in(seeds[3], 71), 0)
    weight = normal_values(seeds[1], (N, OUT), 1.0, 6.0, ((0, 8), (1, 16)))
    pruned = draw_pruned(jax.random.fold_in(seeds[3], 71), 0)
    return {"hessian_inverse": hessian_inverse, "weight": weight, "pruned": pruned}


def contract_rows(gains, rows):
    return lax.dot_general(gains.astype(jnp.float32), rows.astype(jnp.float32), (((0,), (0,)), ((), ())), precision=lax.Precision.HIGHEST, preferred_element_type=jnp.float32)

def solve_pivot(factor, rhs):
    half = lax.linalg.triangular_solve(factor, rhs, left_side=True, lower=True)
    return lax.linalg.triangular_solve(factor, half, left_side=True, lower=True, transpose_a=True)

def reference(hessian_inverse, weight, pruned):
    inverse = hessian_inverse
    slab = weight.astype(jnp.float32)
    for panel in range(PANELS):
        listed = pruned[panel]
        rows = inverse[listed]
        pivot = rows[:, listed]
        factor = jnp.linalg.cholesky(pivot)
        columns = inverse[:, listed]
        gains = solve_pivot(factor, columns.T)
        slab_rows = slab[listed]
        slab = slab - contract_rows(gains, slab_rows)
        slab = slab.at[listed, :].set(0.0)
        inverse = inverse - contract_rows(gains, rows)
        inverse = inverse.at[listed, :].set(0.0).at[:, listed].set(0.0)
    return (inverse, slab.astype(jnp.bfloat16))
```

```python
import functools

import jax
import jax.numpy as jnp
from jax import lax
from jax.experimental import pallas as pl
from jax.experimental.pallas import tpu as pltpu
from jax.sharding import PartitionSpec as P

NB = 128
f32 = jnp.float32
bf16 = jnp.bfloat16


def split(x):
    high = x.astype(bf16)
    return high, (x - high.astype(f32)).astype(bf16)


def dot3(a, b):
    def one(p, q):
        return lax.dot_general(p, q, (((1,), (0,)), ((), ())), preferred_element_type=f32)

    return one(a[0], b[0]) + (one(a[0], b[1]) + one(a[1], b[0]))


def inverse_of_block(D):
    lane = lax.broadcasted_iota(jnp.int32, (8, 128), 1)
    sub = lax.broadcasted_iota(jnp.int32, (8, 128), 0)
    for s in range(16):
        R = D[s]
        inside = (lane >= 8 * s) & (lane < 8 * s + 8)
        cols = [jnp.broadcast_to(R[:, 8 * s + j : 8 * s + j + 1], (8, 128)) for j in range(8)]
        e = {(i, j): jnp.broadcast_to(cols[j][i : i + 1, :], (8, 128)) for i in range(8) for j in range(i, 8)}
        r = [
            jnp.where(inside, jnp.where(lane == 8 * s + i, 1.0, 0.0), jnp.broadcast_to(R[i : i + 1, :], (8, 128)))
            for i in range(8)
        ]
        for k in range(8):
            inv = 1.0 / e[k, k]
            raw = {j: e[k, j] for j in range(k, 8)}
            r[k] = r[k] * inv
            scaled = {j: e[k, j] * inv for j in range(k + 1, 8)}
            for i in range(8):
                if i == k:
                    continue
                f = e[i, k] if i < k else raw[i]
                r[i] = r[i] - f * r[k]
                for j in range(max(k + 1, i), 8):
                    e[i, j] = e[i, j] - f * scaled[j]
            for j in range(k + 1, 8):
                e[k, j] = scaled[j]
        U = r[7]
        for i in range(7):
            U = jnp.where(sub == i, r[i], U)
        for b in range(16):
            if b == s:
                continue
            C = D[b]
            acc = jnp.where(inside, 0.0, C)
            for j in range(8):
                acc = acc - jnp.broadcast_to(C[:, 8 * s + j : 8 * s + j + 1], (8, 128)) * r[j]
            D[b] = acc
        D[s] = U
    return D


def inverse_kernel(blocks, m_ref, o_ref):
    o_ref[...] = m_ref[...]

    def body(k, _):
        o = pl.multiple_of(k * NB, NB)
        here = pl.ds(o, NB)
        D = inverse_of_block([o_ref[pl.ds(o + 8 * b, 8), here] for b in range(16)])
        D = jnp.concatenate(D, axis=0)
        o_ref[here, here] = jnp.zeros((NB, NB), f32)
        d = split(D)
        U = dot3(d, split(o_ref[here, :]))
        o_ref[here, :] = U
        u = split(U)

        def rows(i, _):
            @pl.when(i != k)
            def _():
                there = pl.ds(pl.multiple_of(i * NB, NB), NB)
                c = split(o_ref[there, here])
                o_ref[there, here] = jnp.zeros((NB, NB), f32)
                o_ref[there, :] = o_ref[there, :] - dot3(c, u)
                o_ref[there, here] = -dot3(c, d)

            return 0

        lax.fori_loop(0, blocks, rows, 0)
        o_ref[here, here] = D
        return 0

    lax.fori_loop(0, blocks, body, 0)


def invert(m):
    n = m.shape[0]
    return pl.pallas_call(
        functools.partial(inverse_kernel, n // NB),
        out_shape=jax.ShapeDtypeStruct((n, n), f32),
        in_specs=[pl.BlockSpec(memory_space=pltpu.VMEM)],
        out_specs=pl.BlockSpec(memory_space=pltpu.VMEM),
        compiler_params=pltpu.CompilerParams(vmem_limit_bytes=32 << 20),
        name="invert",
    )(m)


def dot_high(a, b, contract):
    return lax.dot_general(a, b, (contract, ((), ())), precision=lax.Precision.HIGH, preferred_element_type=f32)


def per_device(hessian_inverse, weight, pruned):
    rows, cols = hessian_inverse.shape
    listed = pruned.reshape(-1)
    row_ids = listed - lax.axis_index("row") * rows
    col_ids = listed - lax.axis_index("col") * cols
    row_ok = (row_ids >= 0) & (row_ids < rows)
    col_ok = (col_ids >= 0) & (col_ids < cols)
    row_marked = jnp.any(row_ids[None, :] == jnp.arange(rows)[:, None], axis=1)
    col_marked = jnp.any(col_ids[None, :] == jnp.arange(cols)[:, None], axis=1)
    row_pick = jnp.clip(row_ids, 0, rows - 1)
    col_pick = jnp.clip(col_ids, 0, cols - 1)
    mine = jnp.where(row_ok[:, None], jnp.take(hessian_inverse, row_pick, axis=0), 0.0)
    slab = jnp.where(row_ok[:, None], jnp.take(weight.astype(f32), row_pick, axis=0), 0.0)
    right = lax.psum(jnp.concatenate([mine, slab], axis=1), "row")
    pivot = lax.psum(jnp.where(col_ok[None, :], jnp.take(right[:, :cols], col_pick, axis=1), 0.0), "col")
    left = lax.psum(jnp.where(col_ok[None, :], jnp.take(hessian_inverse, col_pick, axis=1), 0.0), "col")
    solved = dot_high(invert(pivot), right, ((1,), (0,)))
    update = dot_high(left, solved, ((1,), (0,)))
    inverse = jnp.where(row_marked[:, None] | col_marked[None, :], 0.0, hessian_inverse - update[:, :cols])
    slab = jnp.where(row_marked[:, None], 0.0, weight.astype(f32) - update[:, cols:])
    return inverse, slab.astype(bf16)


def solution(mesh):
    in_specs = (P("row", "col"), P("row", "col"), P())
    out_specs = (P("row", "col"), P("row", "col"))
    return jax.shard_map(per_device, mesh=mesh, in_specs=in_specs, out_specs=out_specs, check_vma=False)
```

```python
import functools

import jax
import jax.numpy as jnp
from jax import lax
from jax.experimental import pallas as pl
from jax.experimental.pallas import tpu as pltpu
from jax.sharding import PartitionSpec as P

NB = 128
f32 = jnp.float32
bf16 = jnp.bfloat16


def split(x):
    high = x.astype(bf16)
    return high, (x - high.astype(f32)).astype(bf16)


def dot3(a, b):
    def one(p, q):
        return lax.dot_general(p, q, (((1,), (0,)), ((), ())), preferred_element_type=f32)

    return one(a[0], b[0]) + (one(a[0], b[1]) + one(a[1], b[0]))


def inverse_of_block(D):
    lane = lax.broadcasted_iota(jnp.int32, (8, 128), 1)
    sub = lax.broadcasted_iota(jnp.int32, (8, 128), 0)
    for s in range(16):
        R = D[s]
        inside = (lane >= 8 * s) & (lane < 8 * s + 8)
        cols = [jnp.broadcast_to(R[:, 8 * s + j : 8 * s + j + 1], (8, 128)) for j in range(8)]
        e = {(i, j): jnp.broadcast_to(cols[j][i : i + 1, :], (8, 128)) for i in range(8) for j in range(i, 8)}
        r = [
            jnp.where(inside, jnp.where(lane == 8 * s + i, 1.0, 0.0), jnp.broadcast_to(R[i : i + 1, :], (8, 128)))
            for i in range(8)
        ]
        for k in range(8):
            inv = 1.0 / e[k, k]
            raw = {j: e[k, j] for j in range(k, 8)}
            r[k] = r[k] * inv
            scaled = {j: e[k, j] * inv for j in range(k + 1, 8)}
            for i in range(8):
                if i == k:
                    continue
                f = e[i, k] if i < k else raw[i]
                r[i] = r[i] - f * r[k]
                for j in range(max(k + 1, i), 8):
                    e[i, j] = e[i, j] - f * scaled[j]
            for j in range(k + 1, 8):
                e[k, j] = scaled[j]
        U = r[7]
        for i in range(7):
            U = jnp.where(sub == i, r[i], U)
        for b in range(16):
            if b == s:
                continue
            C = D[b]
            acc = jnp.where(inside, 0.0, C)
            for j in range(8):
                acc = acc - jnp.broadcast_to(C[:, 8 * s + j : 8 * s + j + 1], (8, 128)) * r[j]
            D[b] = acc
        D[s] = U
    return D


def inverse_kernel(blocks, k_ref, mine_ref, other_ref, o_ref):
    half = o_ref.shape[1] // 2
    core = k_ref[0]
    o_ref[:, pl.ds(pl.multiple_of(core * half, 128), half)] = mine_ref[...]
    o_ref[:, pl.ds(pl.multiple_of((1 - core) * half, 128), half)] = other_ref[...]
    eliminate(blocks, 0, CUTS[0], o_ref)


def rest_kernel(blocks, first, last, m_ref, o_ref):
    o_ref[...] = m_ref[...]
    eliminate(blocks, first, last, o_ref)


CUTS = (2, 5)


def eliminate(blocks, first, last, o_ref):
    def body(k, _):
        o = pl.multiple_of(k * NB, NB)
        here = pl.ds(o, NB)
        D = inverse_of_block([o_ref[pl.ds(o + 8 * b, 8), here] for b in range(16)])
        D = jnp.concatenate(D, axis=0)
        o_ref[here, here] = jnp.zeros((NB, NB), f32)
        d = split(D)
        U = dot3(d, split(o_ref[here, :]))
        o_ref[here, :] = U
        u = split(U)

        def rows(i, _):
            @pl.when(i != k)
            def _():
                there = pl.ds(pl.multiple_of(i * NB, NB), NB)
                c = split(o_ref[there, here])
                o_ref[there, here] = jnp.zeros((NB, NB), f32)
                o_ref[there, :] = o_ref[there, :] - dot3(c, u)
                o_ref[there, here] = -dot3(c, d)

            return 0

        lax.fori_loop(0, blocks, rows, 0)
        o_ref[here, here] = D
        return 0

    lax.fori_loop(first, last, body, 0)


VMEM = pl.BlockSpec(memory_space=pltpu.VMEM)
SMEM = pl.BlockSpec(memory_space=pltpu.SMEM)


def invert(core, mine, other):
    n = mine.shape[0]
    return pl.pallas_call(
        functools.partial(inverse_kernel, n // NB),
        out_shape=jax.ShapeDtypeStruct((n, n), f32),
        in_specs=[SMEM, VMEM, VMEM],
        out_specs=VMEM,
        compiler_params=pltpu.CompilerParams(vmem_limit_bytes=32 << 20),
        cost_estimate=pl.CostEstimate(flops=12 * n**3, bytes_accessed=8 * n * n, transcendentals=0),
        name="invert",
    )(core.reshape(1), mine, other)


def invert_rest(m, first, last):
    n = m.shape[0]
    return pl.pallas_call(
        functools.partial(rest_kernel, n // NB, first, last),
        out_shape=jax.ShapeDtypeStruct((n, n), f32),
        in_specs=[VMEM],
        out_specs=VMEM,
        compiler_params=pltpu.CompilerParams(vmem_limit_bytes=32 << 20),
        cost_estimate=pl.CostEstimate(flops=12 * n**3, bytes_accessed=8 * n * n, transcendentals=0),
        name="invert_rest",
    )(m)


def lay(cap, per, meta_ref, refs, scratch, spread):
    width = refs[0].shape[1]
    line = lax.broadcasted_iota(jnp.int32, (cap + 8, 128), 0)
    blank = jnp.zeros((8, 128), f32)
    for a, ref in enumerate(refs):

        def place(i, _):
            slot = a * per + i
            start, count = meta_ref[0, slot], meta_ref[1, slot]
            shift = lax.rem(start, 8)
            to = pl.ds(pl.multiple_of(start - shift, 8), cap + 8)
            inside = (line >= shift) & (line < shift + count)
            base = meta_ref[2, slot] * width if spread else 0
            for t in range(0, width, 128):
                block = ref[pl.ds(pl.multiple_of(i * cap, 8), cap), t : t + 128]
                block = pltpu.roll(jnp.concatenate([block, blank], axis=0), shift, 0)
                across = pl.ds(pl.multiple_of(base + t, 128), 128)
                scratch[to, across] = jnp.where(inside, block, scratch[to, across])
            return 0

        lax.fori_loop(0, per, place, 0)


def pack_kernel(cap, per, transposed, meta_ref, *refs):
    ins, o_ref, scratch = refs[:-2], refs[-2], refs[-1]
    lay(cap, per, meta_ref, ins, scratch, False)
    if transposed:
        rows = o_ref.shape[1]
        start = pl.multiple_of(meta_ref[2, 0] * rows, 128)
        o_ref[...] = scratch[pl.ds(start, rows), :].T[: o_ref.shape[0]]
    else:
        o_ref[...] = scratch[: o_ref.shape[0], :]


def pack(meta, blocks, cap, total, transposed=None):
    per = blocks[0].shape[0] // cap
    width = blocks[0].shape[1]
    shape = transposed or (total, width)
    return pl.pallas_call(
        functools.partial(pack_kernel, cap, per, transposed is not None),
        out_shape=jax.ShapeDtypeStruct(shape, f32),
        in_specs=[SMEM] + [VMEM] * len(blocks),
        out_specs=VMEM,
        scratch_shapes=[pltpu.VMEM((total + cap + 8, width), f32)],
        compiler_params=pltpu.CompilerParams(vmem_limit_bytes=32 << 20),
        name="pack",
    )(meta, *blocks)


TILE = 256


def solve_kernel(cap, meta_ref, x_ref, own_ref, other_ref, high_ref, low_ref, scratch, right_high, right_low):
    n = x_ref.shape[0]
    lay(cap, own_ref.shape[0] // cap, meta_ref, (own_ref, other_ref), scratch, False)

    def cut(i, _):
        here = pl.ds(pl.multiple_of(i * NB, NB), NB)
        right_high[here, :], right_low[here, :] = split(scratch[here, :])
        return 0

    lax.fori_loop(0, n // NB, cut, 0)

    def multiply(i, _):
        here = pl.ds(pl.multiple_of(i * TILE, TILE), TILE)
        tile = dot3(split(x_ref[here, :]), (right_high[...], right_low[...]))
        high_ref[here, :], low_ref[here, :] = split(tile)
        return 0

    lax.fori_loop(0, n // TILE, multiply, 0)


def solve(meta, inverted, own, other, cap):
    n, width = inverted.shape[0], own.shape[1]
    half = jax.ShapeDtypeStruct((n, width), bf16)
    return pl.pallas_call(
        functools.partial(solve_kernel, cap),
        out_shape=(half, half),
        in_specs=[SMEM, VMEM, VMEM, VMEM],
        out_specs=(VMEM, VMEM),
        scratch_shapes=[
            pltpu.VMEM((n + cap + 8, width), f32),
            pltpu.VMEM((n, width), bf16),
            pltpu.VMEM((n, width), bf16),
        ],
        compiler_params=pltpu.CompilerParams(vmem_limit_bytes=40 << 20),
        cost_estimate=pl.CostEstimate(flops=6 * n * n * width, bytes_accessed=14 << 20, transcendentals=0),
        name="solve",
    )(meta, inverted, own, other)


def finish_kernel(cap, n, meta_ref, h_ref, w_ref, row_ref, col_ref, high_ref, low_ref, *refs):
    blocks, h_out, w_out, scratch = refs[:4], refs[4], refs[5], refs[6]
    cols = h_ref.shape[1]

    @pl.when(pl.program_id(0) == 0)
    def _():
        lay(cap, blocks[0].shape[0] // cap, meta_ref, blocks, scratch, True)

    here = pl.ds(pl.multiple_of(pl.program_id(0) * TILE, TILE), TILE)
    update = jnp.zeros((TILE, high_ref.shape[1]), f32)
    for k in range(0, n, TILE):
        left = split(scratch[k : k + TILE, here].T)
        update = update + dot3(left, (high_ref[k : k + TILE, :], low_ref[k : k + TILE, :]))
    row = row_ref[...] > 0.5
    gone = row | (col_ref[...] > 0.5)
    h_out[...] = jnp.where(gone, 0.0, h_ref[...] - update[:, :cols])
    w_out[...] = jnp.where(row, 0.0, w_ref[...].astype(f32) - update[:, cols:]).astype(bf16)


def finish(meta, h, w, row_marked, col_marked, solved, blocks, cap):
    rows, cols = h.shape
    n, width = solved[0].shape
    return pl.pallas_call(
        functools.partial(finish_kernel, cap, n),
        out_shape=(jax.ShapeDtypeStruct(h.shape, f32), jax.ShapeDtypeStruct(w.shape, bf16)),
        grid=(rows // TILE,),
        in_specs=[
            SMEM,
            pl.BlockSpec((TILE, cols), lambda i: (i, 0)),
            pl.BlockSpec((TILE, w.shape[1]), lambda i: (i, 0)),
            pl.BlockSpec((TILE, 1), lambda i: (i, 0)),
            pl.BlockSpec((1, cols), lambda i: (0, 0)),
            VMEM,
            VMEM,
        ]
        + [VMEM] * 4,
        out_specs=(
            pl.BlockSpec((TILE, cols), lambda i: (i, 0)),
            pl.BlockSpec((TILE, w.shape[1]), lambda i: (i, 0)),
        ),
        scratch_shapes=[pltpu.VMEM((n + cap + 8, rows), f32)],
        compiler_params=pltpu.CompilerParams(vmem_limit_bytes=44 << 20),
        cost_estimate=pl.CostEstimate(flops=6 * n * rows * width, bytes_accessed=24 << 20, transcendentals=0),
        name="finish",
    )(meta, h, w, row_marked.astype(f32)[:, None], col_marked.astype(f32)[None, :], *solved, *blocks)


def plain_inverse(m):
    ids = jnp.arange(m.shape[0])

    def step(k, m):
        here = ids == k
        row, col = lax.dynamic_slice(m, (k, 0), (1, m.shape[1])), lax.dynamic_slice(m, (0, k), (m.shape[0], 1))
        row = jnp.where(here[None, :], 1.0, row) / row[0, k]
        m = jnp.where(here[None, :], 0.0, m) - col * row
        return jnp.where(here[:, None], row, m)

    return lax.fori_loop(0, m.shape[0], step, m)


def dot_high(a, b, contract):
    return lax.dot_general(a, b, (contract, ((), ())), precision=lax.Precision.HIGH, preferred_element_type=f32)


SIDE = 4
CAP_ROWS = 176
CAP_COLS = 96
STEPS = (0, 1, 3, 2)
BOTH = ("row", "col")


def move(value, where):
    def number(x, y, z, core):
        return (2 * (z % SIDE) + core % 2) * SIDE * SIDE + (x % SIDE) * SIDE + y % SIDE

    pairs = [
        (number(x, y, z, core), number(*where(x, y, z, core)))
        for x in range(SIDE)
        for y in range(SIDE)
        for z in range(SIDE)
        for core in range(2)
    ]
    return lax.ppermute(value, BOTH, pairs)


def along_z(value):
    return [value] + [move(value, lambda x, y, z, core, d=d: (x, y, z + d, core)) for d in STEPS[1:]]


def first_turn(value):
    return [value] + [
        move(value, lambda x, y, z, core, d=d: (x, y + d, z, core) if core else (x + d, y, z, core)) for d in STEPS[1:]
    ]


def second_turn(value):
    return [value] + [
        move(value, lambda x, y, z, core, d=d: (x + d, y, z, core) if core else (x, y + d, z, core)) for d in STEPS[1:]
    ]


def other_core(value):
    return move(value, lambda x, y, z, core: (x, y, z, core + 1))


def to_plane(value):
    def where(x, y, z, core):
        r, c = 2 * z + core, SIDE * x + y
        row, col = c // 2, (c % 2) * 8 + r
        return col // SIDE, col % SIDE, row // 2, row % 2

    return move(value, where)


def ring_sum(value, axis, count):
    ring = [(i, (i + 1) % count) for i in range(count)]

    def step(_, carry):
        total, passing = carry
        passing = lax.ppermute(passing, axis, ring)
        return total + passing, passing

    return lax.fori_loop(0, count - 1, step, (value, value))[0]


def per_device(counts, hessian_inverse, weight, pruned):
    rows, cols = hessian_inverse.shape
    r, c = lax.axis_index("row"), lax.axis_index("col")
    z, core, x, y = r // 2, r % 2, c // SIDE, c % SIDE
    listed = pruned.reshape(-1)
    n = listed.shape[0]
    rank = jnp.sum((listed[None, :] < listed[:, None]).astype(jnp.int32), axis=1)
    order = jnp.sum(jnp.where(rank[:, None] == jnp.arange(n)[None, :], listed[:, None], 0), axis=0)
    bounds = jnp.sum((listed[:, None] < cols * jnp.arange(counts[1] + 1)[None, :]).astype(jnp.int32), axis=0)
    col_from, col_count = bounds[:-1], bounds[1:] - bounds[:-1]
    row_from, row_count = bounds[:-1:2], bounds[2::2] - bounds[:-1:2]
    fits = (jnp.max(row_count) <= CAP_ROWS) & (jnp.max(col_count) <= CAP_COLS)
    order = jnp.concatenate([order, jnp.full((CAP_ROWS,), -1, jnp.int32)])
    row_pick = jnp.clip(lax.dynamic_slice(order, (row_from[r],), (CAP_ROWS,)) - r * rows, 0, rows - 1)
    col_pick = lax.dynamic_slice(order, (col_from[c],), (128,)) - c * cols
    slab = weight.astype(f32)
    own = jnp.take(hessian_inverse, row_pick, axis=0)
    own_slab = jnp.take(slab, row_pick, axis=0)

    chosen = (jnp.arange(cols)[:, None] == col_pick[None, :]).astype(f32)
    corner = lax.dot_general(
        own, chosen, (((1,), (0,)), ((), ())), precision=lax.Precision.HIGHEST, preferred_element_type=f32
    )
    back = jnp.array(STEPS)
    sources = 2 * ((z - back) % SIDE)
    sources = jnp.concatenate([sources + core, sources + 1 - core])
    row_meta = jnp.stack([row_from[sources], row_count[sources], jnp.full((8,), core)])
    stack = jnp.concatenate(along_z(corner), axis=0)
    strip = pack(row_meta, [stack, other_core(stack)], CAP_ROWS, n, transposed=(CAP_COLS, n // 2))
    first, second = jnp.tile(back, SIDE), jnp.repeat(back, SIDE)
    from_x = (x - jnp.where(core == 0, first, second)) % SIDE
    from_y = (y - jnp.where(core == 0, second, first)) % SIDE
    place = SIDE * from_x + from_y
    col_meta = jnp.stack([col_from[place], col_count[place]])
    half = pack(col_meta, second_turn(jnp.concatenate(first_turn(strip), axis=0)), CAP_COLS, n)
    other_half = other_core(half)
    inverted = invert(core, half, other_half)
    inverted = invert_rest(inverted, *CUTS)
    inverted = invert_rest(inverted, CUTS[1], n // NB)

    stack = jnp.concatenate(along_z(jnp.concatenate([own, own_slab], axis=1)), axis=0)
    solved = solve(row_meta, inverted, stack, other_core(stack), CAP_ROWS)
    plane_meta = jnp.stack([row_from[place % 8], row_count[place % 8], place // 8])
    gathered = second_turn(jnp.concatenate(first_turn(to_plane(own)), axis=0))

    row_ids, col_ids = listed - r * rows, listed - c * cols
    row_marked = jnp.any(row_ids[None, :] == jnp.arange(rows)[:, None], axis=1)
    col_marked = jnp.any(col_ids[None, :] == jnp.arange(cols)[:, None], axis=1)
    done = finish(
        plane_meta, hessian_inverse, weight, row_marked, col_marked, solved, gathered, CAP_ROWS
    )

    def anywhere(_):
        row_ok = (row_ids >= 0) & (row_ids < rows)
        both = jnp.concatenate([hessian_inverse, slab], axis=1)
        mine = jnp.where(row_ok[:, None], jnp.take(both, jnp.clip(row_ids, 0, rows - 1), axis=0), 0.0)
        right = ring_sum(mine, "row", counts[0])
        inside = (jnp.arange(cols)[:, None] == col_ids[None, :]).astype(f32)

        def pick(a):
            return lax.dot_general(
                a, inside, (((1,), (0,)), ((), ())), precision=lax.Precision.HIGHEST, preferred_element_type=f32
            )

        pivot = ring_sum(pick(right[:, :cols]), "col", counts[1])
        left = ring_sum(pick(hessian_inverse).T, "col", counts[1])
        solved = dot_high(plain_inverse(pivot), right, ((1,), (0,)))
        changed = hessian_inverse - dot_high(left, solved[:, :cols], ((0,), (0,)))
        slab_changed = slab - dot_high(left, solved[:, cols:], ((0,), (0,)))
        inverse = jnp.where(row_marked[:, None] | col_marked[None, :], 0.0, changed)
        return inverse, jnp.where(row_marked[:, None], 0.0, slab_changed).astype(bf16)

    return lax.cond(fits, lambda done: done, anywhere, done)


def solution(mesh):
    in_specs = (P("row", "col"), P("row", "col"), P())
    out_specs = (P("row", "col"), P("row", "col"))
    counts = (mesh.shape["row"], mesh.shape["col"])

    def body(*args):
        return per_device(counts, *args)

    return jax.shard_map(body, mesh=mesh, in_specs=in_specs, out_specs=out_specs, check_vma=False)
```

```python
import functools

import jax
import jax.numpy as jnp
from jax import lax
from jax.experimental import pallas as pl
from jax.experimental.pallas import tpu as pltpu
from jax.sharding import PartitionSpec as P

NB = 128
f32 = jnp.float32
bf16 = jnp.bfloat16


def split(x):
    high = x.astype(bf16)
    return high, (x - high.astype(f32)).astype(bf16)


def dot3(a, b):
    left = jnp.concatenate([a[0], a[0], a[1]], axis=1)
    right = jnp.concatenate([b[0], b[1], b[0]], axis=0)
    return lax.dot_general(left, right, (((1,), (0,)), ((), ())), preferred_element_type=f32)


def inverse_of_block(D):
    lane = lax.broadcasted_iota(jnp.int32, (8, 128), 1)
    sub = lax.broadcasted_iota(jnp.int32, (8, 128), 0)
    for s in range(16):
        R = D[s]
        inside = (lane >= 8 * s) & (lane < 8 * s + 8)
        cols = [jnp.broadcast_to(R[:, 8 * s + j : 8 * s + j + 1], (8, 128)) for j in range(8)]
        e = {(i, j): jnp.broadcast_to(cols[j][i : i + 1, :], (8, 128)) for i in range(8) for j in range(i, 8)}
        r = [
            jnp.where(inside, jnp.where(lane == 8 * s + i, 1.0, 0.0), jnp.broadcast_to(R[i : i + 1, :], (8, 128)))
            for i in range(8)
        ]
        for k in range(8):
            inv = 1.0 / e[k, k]
            raw = {j: e[k, j] for j in range(k, 8)}
            r[k] = r[k] * inv
            scaled = {j: e[k, j] * inv for j in range(k + 1, 8)}
            for i in range(8):
                if i == k:
                    continue
                f = e[i, k] if i < k else raw[i]
                r[i] = r[i] - f * r[k]
                for j in range(max(k + 1, i), 8):
                    e[i, j] = e[i, j] - f * scaled[j]
            for j in range(k + 1, 8):
                e[k, j] = scaled[j]
        U = r[7]
        for i in range(7):
            U = jnp.where(sub == i, r[i], U)
        for b in range(16):
            if b == s:
                continue
            C = D[b]
            acc = jnp.where(inside, 0.0, C)
            for j in range(8):
                acc = acc - jnp.broadcast_to(C[:, 8 * s + j : 8 * s + j + 1], (8, 128)) * r[j]
            D[b] = acc
        D[s] = U
    return D


def inverse_kernel(blocks, k_ref, mine_ref, other_ref, o_ref, *scratch):
    half = o_ref.shape[1] // 2
    core = k_ref[0]
    o_ref[:, pl.ds(pl.multiple_of(core * half, 128), half)] = mine_ref[...]
    o_ref[:, pl.ds(pl.multiple_of((1 - core) * half, 128), half)] = other_ref[...]
    eliminate(blocks, 0, CUTS[0], o_ref, *scratch)


def rest_kernel(blocks, first, last, m_ref, o_ref, *scratch):
    o_ref[...] = m_ref[...]
    eliminate(blocks, first, last, o_ref, *scratch)


CUTS = (2, 5)


def eliminate(blocks, first, last, o_ref, c_ref, u_ref):
    def body(k, _):
        o = pl.multiple_of(k * NB, NB)
        here = pl.ds(o, NB)
        D = inverse_of_block([o_ref[pl.ds(o + 8 * b, 8), here] for b in range(16)])
        D = jnp.concatenate(D, axis=0)

        def panel(i, _):
            there = pl.ds(pl.multiple_of(i * NB, NB), NB)
            high, low = split(jnp.where(i == k, 0.0, o_ref[there, here]))
            c_ref[there, :] = jnp.concatenate([high, high, low], axis=1)
            o_ref[there, here] = jnp.zeros((NB, NB), f32)
            return 0

        U = dot3(split(D), split(o_ref[here, :]))
        lax.fori_loop(0, blocks, panel, 0, unroll=True)
        o_ref[here, :] = U
        o_ref[here, here] = D
        high, low = split(o_ref[here, :])
        u_ref[...] = jnp.concatenate([high, low, high], axis=0)

        def rows(i, _):
            there = pl.ds(pl.multiple_of(i * 2 * NB, 2 * NB), 2 * NB)
            o_ref[there, :] = o_ref[there, :] - jnp.dot(c_ref[there, :], u_ref[...], preferred_element_type=f32)
            return 0

        lax.fori_loop(0, blocks // 2, rows, 0)
        return 0

    lax.fori_loop(first, last, body, 0)


VMEM = pl.BlockSpec(memory_space=pltpu.VMEM)
SMEM = pl.BlockSpec(memory_space=pltpu.SMEM)


def invert(core, mine, other):
    n = mine.shape[0]
    return pl.pallas_call(
        functools.partial(inverse_kernel, n // NB),
        out_shape=jax.ShapeDtypeStruct((n, n), f32),
        in_specs=[SMEM, VMEM, VMEM],
        out_specs=VMEM,
        scratch_shapes=[pltpu.VMEM((n, 3 * NB), bf16), pltpu.VMEM((3 * NB, n), bf16)],
        compiler_params=pltpu.CompilerParams(vmem_limit_bytes=32 << 20),
        cost_estimate=pl.CostEstimate(flops=12 * n**3, bytes_accessed=8 * n * n, transcendentals=0),
        name="invert",
    )(core.reshape(1), mine, other)


def invert_rest(m, first, last):
    n = m.shape[0]
    return pl.pallas_call(
        functools.partial(rest_kernel, n // NB, first, last),
        out_shape=jax.ShapeDtypeStruct((n, n), f32),
        in_specs=[VMEM],
        out_specs=VMEM,
        scratch_shapes=[pltpu.VMEM((n, 3 * NB), bf16), pltpu.VMEM((3 * NB, n), bf16)],
        compiler_params=pltpu.CompilerParams(vmem_limit_bytes=32 << 20),
        cost_estimate=pl.CostEstimate(flops=12 * n**3, bytes_accessed=8 * n * n, transcendentals=0),
        name="invert_rest",
    )(m)


def lay(cap, per, meta_ref, refs, scratch, spread):
    width = refs[0].shape[1]
    line = lax.broadcasted_iota(jnp.int32, (cap + 8, 128), 0)
    blank = jnp.zeros((8, 128), f32)
    for a, ref in enumerate(refs):

        def place(i, _):
            slot = a * per + i
            start, count = meta_ref[0, slot], meta_ref[1, slot]
            shift = lax.rem(start, 8)
            to = pl.ds(pl.multiple_of(start - shift, 8), cap + 8)
            inside = (line >= shift) & (line < shift + count)
            base = meta_ref[2, slot] * width if spread else 0
            for t in range(0, width, 128):
                block = ref[pl.ds(pl.multiple_of(i * cap, 8), cap), t : t + 128]
                block = pltpu.roll(jnp.concatenate([block, blank], axis=0), shift, 0)
                across = pl.ds(pl.multiple_of(base + t, 128), 128)
                scratch[to, across] = jnp.where(inside, block, scratch[to, across])
            return 0

        lax.fori_loop(0, per, place, 0)


def pack_kernel(cap, per, transposed, meta_ref, *refs):
    ins, o_ref, scratch = refs[:-2], refs[-2], refs[-1]
    lay(cap, per, meta_ref, ins, scratch, False)
    if transposed:
        rows = o_ref.shape[1]
        start = pl.multiple_of(meta_ref[2, 0] * rows, 128)
        o_ref[...] = scratch[pl.ds(start, rows), :].T[: o_ref.shape[0]]
    else:
        o_ref[...] = scratch[: o_ref.shape[0], :]


def pack(meta, blocks, cap, total, transposed=None):
    per = blocks[0].shape[0] // cap
    width = blocks[0].shape[1]
    shape = transposed or (total, width)
    return pl.pallas_call(
        functools.partial(pack_kernel, cap, per, transposed is not None),
        out_shape=jax.ShapeDtypeStruct(shape, f32),
        in_specs=[SMEM] + [VMEM] * len(blocks),
        out_specs=VMEM,
        scratch_shapes=[pltpu.VMEM((total + cap + 8, width), f32)],
        compiler_params=pltpu.CompilerParams(vmem_limit_bytes=32 << 20),
        name="pack",
    )(meta, *blocks)


TILE = 256


def solve_kernel(cap, meta_ref, x_ref, own_ref, other_ref, high_ref, low_ref, scratch, right_high, right_low):
    n = x_ref.shape[0]
    lay(cap, own_ref.shape[0] // cap, meta_ref, (own_ref, other_ref), scratch, False)

    def cut(i, _):
        here = pl.ds(pl.multiple_of(i * NB, NB), NB)
        right_high[here, :], right_low[here, :] = split(scratch[here, :])
        return 0

    lax.fori_loop(0, n // NB, cut, 0)

    def multiply(i, _):
        here = pl.ds(pl.multiple_of(i * TILE, TILE), TILE)
        tile = dot3(split(x_ref[here, :]), (right_high[...], right_low[...]))
        high_ref[here, :], low_ref[here, :] = split(tile)
        return 0

    lax.fori_loop(0, n // TILE, multiply, 0)


def solve(meta, inverted, own, other, cap):
    n, width = inverted.shape[0], own.shape[1]
    half = jax.ShapeDtypeStruct((n, width), bf16)
    return pl.pallas_call(
        functools.partial(solve_kernel, cap),
        out_shape=(half, half),
        in_specs=[SMEM, VMEM, VMEM, VMEM],
        out_specs=(VMEM, VMEM),
        scratch_shapes=[
            pltpu.VMEM((n + cap + 8, width), f32),
            pltpu.VMEM((n, width), bf16),
            pltpu.VMEM((n, width), bf16),
        ],
        compiler_params=pltpu.CompilerParams(vmem_limit_bytes=40 << 20),
        cost_estimate=pl.CostEstimate(flops=6 * n * n * width, bytes_accessed=14 << 20, transcendentals=0),
        name="solve",
    )(meta, inverted, own, other)


def finish_kernel(cap, n, meta_ref, h_ref, w_ref, row_ref, col_ref, high_ref, low_ref, *refs):
    blocks, h_out, w_out, scratch = refs[:4], refs[4], refs[5], refs[6]
    cols = h_ref.shape[1]

    @pl.when(pl.program_id(0) == 0)
    def _():
        lay(cap, blocks[0].shape[0] // cap, meta_ref, blocks, scratch, True)

    here = pl.ds(pl.multiple_of(pl.program_id(0) * TILE, TILE), TILE)
    update = dot3(split(scratch[:n, here].T), (high_ref[...], low_ref[...]))
    row = row_ref[...] > 0.5
    gone = row | (col_ref[...] > 0.5)
    h_out[...] = jnp.where(gone, 0.0, h_ref[...] - update[:, :cols])
    w_out[...] = jnp.where(row, 0.0, w_ref[...].astype(f32) - update[:, cols:]).astype(bf16)


def finish(meta, h, w, row_marked, col_marked, solved, blocks, cap):
    rows, cols = h.shape
    n, width = solved[0].shape
    return pl.pallas_call(
        functools.partial(finish_kernel, cap, n),
        out_shape=(jax.ShapeDtypeStruct(h.shape, f32), jax.ShapeDtypeStruct(w.shape, bf16)),
        grid=(rows // TILE,),
        in_specs=[
            SMEM,
            pl.BlockSpec((TILE, cols), lambda i: (i, 0)),
            pl.BlockSpec((TILE, w.shape[1]), lambda i: (i, 0)),
            pl.BlockSpec((TILE, 1), lambda i: (i, 0)),
            pl.BlockSpec((1, cols), lambda i: (0, 0)),
            VMEM,
            VMEM,
        ]
        + [VMEM] * 4,
        out_specs=(
            pl.BlockSpec((TILE, cols), lambda i: (i, 0)),
            pl.BlockSpec((TILE, w.shape[1]), lambda i: (i, 0)),
        ),
        scratch_shapes=[pltpu.VMEM((n + cap + 8, rows), f32)],
        compiler_params=pltpu.CompilerParams(vmem_limit_bytes=44 << 20),
        cost_estimate=pl.CostEstimate(flops=6 * n * rows * width, bytes_accessed=24 << 20, transcendentals=0),
        name="finish",
    )(meta, h, w, row_marked.astype(f32)[:, None], col_marked.astype(f32)[None, :], *solved, *blocks)


def plain_inverse(m):
    ids = jnp.arange(m.shape[0])

    def step(k, m):
        here = ids == k
        row, col = lax.dynamic_slice(m, (k, 0), (1, m.shape[1])), lax.dynamic_slice(m, (0, k), (m.shape[0], 1))
        row = jnp.where(here[None, :], 1.0, row) / row[0, k]
        m = jnp.where(here[None, :], 0.0, m) - col * row
        return jnp.where(here[:, None], row, m)

    return lax.fori_loop(0, m.shape[0], step, m)


def dot_high(a, b, contract):
    return lax.dot_general(a, b, (contract, ((), ())), precision=lax.Precision.HIGH, preferred_element_type=f32)


SIDE = 4
CAP_ROWS = 176
CAP_COLS = 96
STEPS = (0, 1, 3, 2)
BOTH = ("row", "col")


def move(value, where):
    def number(x, y, z, core):
        return (2 * (z % SIDE) + core % 2) * SIDE * SIDE + (x % SIDE) * SIDE + y % SIDE

    pairs = [
        (number(x, y, z, core), number(*where(x, y, z, core)))
        for x in range(SIDE)
        for y in range(SIDE)
        for z in range(SIDE)
        for core in range(2)
    ]
    return lax.ppermute(value, BOTH, pairs)


def along_z(value):
    return [value] + [move(value, lambda x, y, z, core, d=d: (x, y, z + d, core)) for d in STEPS[1:]]


def first_turn(value):
    return [value] + [
        move(value, lambda x, y, z, core, d=d: (x, y + d, z, core) if core else (x + d, y, z, core)) for d in STEPS[1:]
    ]


def second_turn(value):
    return [value] + [
        move(value, lambda x, y, z, core, d=d: (x + d, y, z, core) if core else (x, y + d, z, core)) for d in STEPS[1:]
    ]


def other_core(value):
    return move(value, lambda x, y, z, core: (x, y, z, core + 1))


def to_plane(value):
    def where(x, y, z, core):
        r, c = 2 * z + core, SIDE * x + y
        row, col = c // 2, (c % 2) * 8 + r
        return col // SIDE, col % SIDE, row // 2, row % 2

    return move(value, where)


def ring_sum(value, axis, count):
    ring = [(i, (i + 1) % count) for i in range(count)]

    def step(_, carry):
        total, passing = carry
        passing = lax.ppermute(passing, axis, ring)
        return total + passing, passing

    return lax.fori_loop(0, count - 1, step, (value, value))[0]


def per_device(counts, hessian_inverse, weight, pruned):
    rows, cols = hessian_inverse.shape
    r, c = lax.axis_index("row"), lax.axis_index("col")
    z, core, x, y = r // 2, r % 2, c // SIDE, c % SIDE
    listed = pruned.reshape(-1)
    n = listed.shape[0]
    rank = jnp.sum((listed[None, :] < listed[:, None]).astype(jnp.int32), axis=1)
    order = jnp.sum(jnp.where(rank[:, None] == jnp.arange(n)[None, :], listed[:, None], 0), axis=0)
    bounds = jnp.sum((listed[:, None] < cols * jnp.arange(counts[1] + 1)[None, :]).astype(jnp.int32), axis=0)
    col_from, col_count = bounds[:-1], bounds[1:] - bounds[:-1]
    row_from, row_count = bounds[:-1:2], bounds[2::2] - bounds[:-1:2]
    fits = (jnp.max(row_count) <= CAP_ROWS) & (jnp.max(col_count) <= CAP_COLS)
    order = jnp.concatenate([order, jnp.full((CAP_ROWS,), -1, jnp.int32)])
    row_pick = jnp.clip(lax.dynamic_slice(order, (row_from[r],), (CAP_ROWS,)) - r * rows, 0, rows - 1)
    col_pick = lax.dynamic_slice(order, (col_from[c],), (128,)) - c * cols
    slab = weight.astype(f32)
    own = jnp.take(hessian_inverse, row_pick, axis=0)
    own_slab = jnp.take(slab, row_pick, axis=0)

    chosen = (jnp.arange(cols)[:, None] == col_pick[None, :]).astype(f32)
    corner = lax.dot_general(
        own, chosen, (((1,), (0,)), ((), ())), precision=lax.Precision.HIGHEST, preferred_element_type=f32
    )
    back = jnp.array(STEPS)
    sources = 2 * ((z - back) % SIDE)
    sources = jnp.concatenate([sources + core, sources + 1 - core])
    row_meta = jnp.stack([row_from[sources], row_count[sources], jnp.full((8,), core)])
    stack = jnp.concatenate(along_z(corner), axis=0)
    strip = pack(row_meta, [stack, other_core(stack)], CAP_ROWS, n, transposed=(CAP_COLS, n // 2))
    first, second = jnp.tile(back, SIDE), jnp.repeat(back, SIDE)
    from_x = (x - jnp.where(core == 0, first, second)) % SIDE
    from_y = (y - jnp.where(core == 0, second, first)) % SIDE
    place = SIDE * from_x + from_y
    col_meta = jnp.stack([col_from[place], col_count[place]])
    strips = second_turn(jnp.concatenate(first_turn(strip), axis=0))
    half = pack(col_meta, strips, CAP_COLS, n)
    other_half = other_core(half)
    inverted = invert(core, half, other_half)
    inverted = invert_rest(inverted, *CUTS)
    inverted = invert_rest(inverted, CUTS[1], n // NB)

    stack = jnp.concatenate(along_z(jnp.concatenate([own, own_slab], axis=1)), axis=0)
    solved = solve(row_meta, inverted, stack, other_core(stack), CAP_ROWS)
    plane_meta = jnp.stack([row_from[place % 8], row_count[place % 8], place // 8])
    gathered = second_turn(jnp.concatenate(first_turn(to_plane(own)), axis=0))

    row_ids, col_ids = listed - r * rows, listed - c * cols
    row_marked = jnp.any(row_ids[None, :] == jnp.arange(rows)[:, None], axis=1)
    col_marked = jnp.any(col_ids[None, :] == jnp.arange(cols)[:, None], axis=1)
    done = finish(
        plane_meta, hessian_inverse, weight, row_marked, col_marked, solved, gathered, CAP_ROWS
    )

    def anywhere(_):
        row_ok = (row_ids >= 0) & (row_ids < rows)
        both = jnp.concatenate([hessian_inverse, slab], axis=1)
        mine = jnp.where(row_ok[:, None], jnp.take(both, jnp.clip(row_ids, 0, rows - 1), axis=0), 0.0)
        right = ring_sum(mine, "row", counts[0])
        inside = (jnp.arange(cols)[:, None] == col_ids[None, :]).astype(f32)

        def pick(a):
            return lax.dot_general(
                a, inside, (((1,), (0,)), ((), ())), precision=lax.Precision.HIGHEST, preferred_element_type=f32
            )

        pivot = ring_sum(pick(right[:, :cols]), "col", counts[1])
        left = ring_sum(pick(hessian_inverse).T, "col", counts[1])
        solved = dot_high(plain_inverse(pivot), right, ((1,), (0,)))
        changed = hessian_inverse - dot_high(left, solved[:, :cols], ((0,), (0,)))
        slab_changed = slab - dot_high(left, solved[:, cols:], ((0,), (0,)))
        inverse = jnp.where(row_marked[:, None] | col_marked[None, :], 0.0, changed)
        return inverse, jnp.where(row_marked[:, None], 0.0, slab_changed).astype(bf16)

    return lax.cond(fits, lambda done: done, anywhere, done)


def solution(mesh):
    in_specs = (P("row", "col"), P("row", "col"), P())
    out_specs = (P("row", "col"), P("row", "col"))
    counts = (mesh.shape["row"], mesh.shape["col"])

    def body(*args):
        return per_device(counts, *args)

    return jax.shard_map(body, mesh=mesh, in_specs=in_specs, out_specs=out_specs, check_vma=False)
```
